32 devices in a mesh: blk: 8 (over z, x), mp: 4 (over y, core).
Axes of the slice: x: 2, y: 2, z: 4, core: 2. Of those that a mesh axis runs over, the one named last changes fastest.
Arguments:
- tokens: bfloat16 [8, 320, 7168], P('blk', 'mp'), may hold values from -6 to 6
- cotangent: bfloat16 [8, 320, 7168], P('blk', 'mp'), may hold values from -6 to 6
- gate_weight: bfloat16 [8, 7168, 512], P('blk', None, 'mp'), may hold values from -6 to 6
- up_weight: bfloat16 [8, 7168, 512], P('blk', None, 'mp'), may hold values from -6 to 6
- down_weight: bfloat16 [8, 512, 7168], P('blk', 'mp'), may hold values from -6 to 6
- mass: float32 [8], P('blk'), may hold values from 0.25 to 4
Outputs:
- gate_next: bfloat16 [8, 7168, 512], P('blk', None, 'mp')
- up_next: bfloat16 [8, 7168, 512], P('blk', None, 'mp')
- down_next: bfloat16 [8, 512, 7168], P('blk', 'mp')
- mass_next: float32 [8], P('blk')
- mass_total: float32 [], replicated
The draws below stay inside these ranges and needn't reach their ends.
All inputs are finite; a program needn't handle non-finite values.
Results may differ from the reference program's by a relative error of at most 0.0051.
Values may be sent and summed in bfloat16 or wider, within the bound.
A program may use at most 128 MiB of HBM per device.

```python
import math
import jax
import jax.numpy as jnp
from jax import lax

D = 7168
TOK = 320
HID = 512
REPLICAS = 8


def level_of(stream_key, extent, cuts, low, top_value):
    level, own = 1.0, jax.random.fold_in(stream_key, 6)
    for axis_at, parts in cuts:
        steps = jnp.exp(jax.random.uniform(jax.random.fold_in(own, axis_at), (parts,), jnp.float32, low / len(cuts), top_value / len(cuts)))
        level = level * jnp.repeat(steps, extent[axis_at] // parts).reshape([-1 if axis == axis_at else 1 for axis in range(len(extent))])
    return level


def gaussian(stream_key, dims, spread, most, pieces=(), kind=jnp.bfloat16):
    result = spread * jax.random.normal(stream_key, dims, jnp.float32)
    if pieces:
        result = result * level_of(stream_key, dims, pieces, -0.22, 0.18)
    return jnp.clip(result, -most, most).astype(kind)


def setup_inputs(seed: int = 0) -> dict:
    splits = jax.random.split(jax.random.key(seed), 7)
    return {
        "tokens": gaussian(splits[0], (REPLICAS, TOK, D), 1.0, 6.0, ((0, 8), (1, 4))),
        "cotangent": gaussian(splits[1], (REPLICAS, TOK, D), 1.0, 6.0, ((0, 8), (1, 4))),
        "gate_weight": gaussian(splits[2], (REPLICAS, D, HID), 1.0, 6.0, ((0, 8), (2, 4))),
        "up_weight": gaussian(splits[3], (REPLICAS, D, HID), 1.0, 6.0, ((0, 8), (2, 4))),
        "down_weight": gaussian(splits[4], (REPLICAS, HID, D), 1.0, 6.0, ((0, 8), (1, 4))),
        "mass": jnp.clip(jnp.exp(math.log(4.0) - 2.7725887 * jax.random.uniform(splits[5], (REPLICAS,), jnp.float32) ** level_of(splits[5], (REPLICAS,), ((0, 8),), -0.2, 0.2)), 0.25, 4.0),
    }


step_size = 0.5


def replica_numerators(x, dy, wg, wu, wd, weight):
    inv_d = D ** -0.5
    inv_h = HID ** -0.5
    gate_pre = jnp.dot(x, wg, preferred_element_type=jnp.float32) * inv_d
    up_pre = jnp.dot(x, wu, preferred_element_type=jnp.float32) * inv_d
    sig = jax.nn.sigmoid(gate_pre)
    hidden = (gate_pre * sig * up_pre).astype(jnp.bfloat16)
    hidden_grad = jnp.dot(dy, wd.T, preferred_element_type=jnp.float32) * inv_h
    gate_gp = (hidden_grad * up_pre * sig * (1.0 + gate_pre * (1.0 - sig))).astype(jnp.bfloat16)
    up_gp = (hidden_grad * gate_pre * sig).astype(jnp.bfloat16)
    gate_grad = jnp.dot(x.T, gate_gp, preferred_element_type=jnp.float32) * inv_d
    up_grad = jnp.dot(x.T, up_gp, preferred_element_type=jnp.float32) * inv_d
    down_grad = jnp.dot(hidden.T, dy, preferred_element_type=jnp.float32) * inv_h
    numer_gate = (weight * (wg.astype(jnp.float32) - step_size * gate_grad)).astype(jnp.bfloat16)
    numer_up = (weight * (wu.astype(jnp.float32) - step_size * up_grad)).astype(jnp.bfloat16)
    numer_down = (weight * (wd.astype(jnp.float32) - step_size * down_grad)).astype(jnp.bfloat16)
    return numer_gate, numer_up, numer_down


def reference(tokens, cotangent, gate_weight, up_weight, down_weight, mass):
    def one(index):
        return replica_numerators(tokens[index], cotangent[index], gate_weight[index],
                                  up_weight[index], down_weight[index], mass[index])

    numer_gate, numer_up, numer_down = lax.map(one, jnp.arange(REPLICAS, dtype=jnp.int32))
    mass_next = (mass + 3.0 * jnp.roll(mass, 1) + 3.0 * jnp.roll(mass, 2) + jnp.roll(mass, 3)) / 8.0

    def mix(index):
        outs = []
        for numer in (numer_gate, numer_up, numer_down):
            first = numer[(index - 1) % REPLICAS].astype(jnp.float32)
            second = numer[(index - 2) % REPLICAS].astype(jnp.float32)
            third = numer[(index - 3) % REPLICAS].astype(jnp.float32)
            total = numer[index].astype(jnp.float32) + 3.0 * first + 3.0 * second + third
            outs.append(((total / 8.0) / mass_next[index]).astype(jnp.bfloat16))
        return tuple(outs)

    gate_next, up_next, down_next = lax.map(mix, jnp.arange(REPLICAS, dtype=jnp.int32))
    mass_total = jnp.sum(mass_next)
    return gate_next, up_next, down_next, mass_next, mass_total
```

```python
import functools

import jax
import jax.numpy as jnp
from jax import lax
from jax.experimental import pallas as pl
from jax.experimental.pallas import tpu as pltpu
from jax.sharding import PartitionSpec as P

step_size = 0.5
MESH = pl.DeviceIdType.MESH
f32 = jnp.float32
bf16 = jnp.bfloat16


def largest_cut(width, most):
    return max(c for c in range(1, most + 1) if width % (c * 128) == 0)


def kernel(
    reps, mp, pieces, chunks,
    tok, cot, wg, wu, wd, mass_s, mass_v,
    gate_o, up_o, down_o, mass_o,
    xy, wgu, wdv, nb, eb, cb, sb, rb, mbuf, acc_gu, acc_h, gpre, hid_t,
    load_sem, own_send, own_recv, far_send, far_recv, fwd_send, fwd_recv,
    m_send, m_recv, e_send, e_recv, c1_send, c_send, c_recv, s_send, r_recv, o_sem,
):
    me = lax.axis_index("blk")
    my = lax.axis_index("mp")
    rows = tok.shape[0]
    width = tok.shape[1]
    units = wg.shape[1]
    inv_d = width ** (-0.5)
    inv_h = (units * mp) ** (-0.5)
    piece = width // pieces
    span = width // chunks
    far = mp // 2 - 1
    odd = lax.rem(me, 2) == 1
    even = lax.rem(me, 2) == 0
    partner = me + 1 - 2 * lax.rem(me, 2)
    ahead = lax.rem(me + 2, reps)
    sibling = my + 1 - 2 * lax.rem(my, 2)

    sources = (tok, cot)
    loads = [
        pltpu.make_async_copy(wg, wgu.at[:, pl.ds(0, units)], load_sem.at[0]),
        pltpu.make_async_copy(wu, wgu.at[:, pl.ds(units, units)], load_sem.at[1]),
        pltpu.make_async_copy(wd, wdv, load_sem.at[2]),
    ]
    mine = pl.ds(pl.multiple_of(my * rows, rows), rows)
    for a in range(2):
        loads.append(pltpu.make_async_copy(sources[a], xy.at[a, mine, :], load_sem.at[3 + a]))
    for load in loads:
        load.start()

    barrier = pltpu.get_barrier_semaphore()

    def greet_blk(d, carry):
        pl.semaphore_signal(
            barrier, inc=1, device_id={"blk": lax.rem(me + d, reps)}, device_id_type=MESH
        )
        return carry

    def greet_mp(d, carry):
        pl.semaphore_signal(
            barrier, inc=1, device_id={"mp": lax.rem(my + d, mp)}, device_id_type=MESH
        )
        return carry

    lax.fori_loop(1, reps, greet_blk, 0)
    lax.fori_loop(1, mp, greet_mp, 0)
    pl.semaphore_wait(barrier, reps - 1 + mp - 1)

    def cols_of(p):
        return pl.ds(pl.multiple_of(p * piece, 128), piece)

    def rows_of(owner):
        return pl.ds(pl.multiple_of(owner * rows, rows), rows)

    def own_copy(a, p):
        return pltpu.make_async_remote_copy(
            src_ref=sources[a].at[:, cols_of(p)],
            dst_ref=xy.at[a, mine, cols_of(p)],
            send_sem=own_send.at[a, p],
            recv_sem=own_recv.at[a, p],
            device_id={"mp": sibling},
            device_id_type=MESH,
        )

    def far_copy(a, q, p):
        return pltpu.make_async_remote_copy(
            src_ref=sources[a].at[:, cols_of(p)],
            dst_ref=xy.at[a, mine, cols_of(p)],
            send_sem=far_send.at[a, q, p],
            recv_sem=far_recv.at[a, q, p],
            device_id={"mp": lax.rem(my + 2 * (q + 1), mp)},
            device_id_type=MESH,
        )

    def fwd_copy(a, q, p):
        owner = lax.rem(my + mp - 2 * (q + 1), mp)
        block = xy.at[a, rows_of(owner), cols_of(p)]
        return pltpu.make_async_remote_copy(
            src_ref=block,
            dst_ref=block,
            send_sem=fwd_send.at[a, q, p],
            recv_sem=fwd_recv.at[a, q, p],
            device_id={"mp": sibling},
            device_id_type=MESH,
        )

    def issue(p, carry):
        for a in range(2):
            for q in range(far):
                far_copy(a, q, p).start()
            own_copy(a, p).start()
        return carry

    lax.fori_loop(0, pieces, issue, 0)

    def mass_copy(d):
        return pltpu.make_async_remote_copy(
            src_ref=mass_v,
            dst_ref=mbuf.at[me],
            send_sem=m_send.at[d],
            recv_sem=m_recv.at[d],
            device_id={"blk": lax.rem(me + d, reps)},
            device_id_type=MESH,
        )

    def mass_start(d, carry):
        mass_copy(d).start()
        return carry

    lax.fori_loop(1, reps, mass_start, 0)
    mbuf[me] = mass_v[...]

    acc_gu[...] = jnp.zeros_like(acc_gu)
    acc_h[...] = jnp.zeros_like(acc_h)
    for load in loads:
        load.wait()

    def gather_step(t, carry):
        @pl.when(t < pieces)
        def _():
            for a in range(2):
                for q in range(far):
                    far_copy(a, q, t).wait_recv()
                    fwd_copy(a, q, t).start()

        @pl.when(t >= 1)
        def _():
            p = t - 1
            for a in range(2):
                own_copy(a, p).wait_recv()
                for q in range(far):
                    fwd_copy(a, q, p).wait_recv()
            cols = cols_of(p)
            acc_gu[...] += jnp.dot(xy[0, :, cols], wgu[cols, :], preferred_element_type=f32)
            acc_h[...] += lax.dot_general(
                xy[1, :, cols], wdv[:, cols], (((1,), (1,)), ((), ())),
                preferred_element_type=f32,
            )

        return carry

    lax.fori_loop(0, pieces + 1, gather_step, 0)

    gate_pre = acc_gu[:, :units] * inv_d
    up_pre = acc_gu[:, units:] * inv_d
    sig = jax.nn.sigmoid(gate_pre)
    hidden = gate_pre * sig * up_pre
    hid_t[...] = hidden.T.astype(bf16)
    hidden_grad = acc_h[...] * inv_h
    gpre[:, :units] = (hidden_grad * up_pre * sig * (1.0 + gate_pre * (1.0 - sig))).astype(bf16)
    gpre[:, units:] = (hidden_grad * gate_pre * sig).astype(bf16)

    def mass_wait(d, carry):
        mass_copy(d).wait()
        return carry

    lax.fori_loop(1, reps, mass_wait, 0)
    mass_next = (
        mbuf[me]
        + 3.0 * mbuf[lax.rem(me + reps - 1, reps)]
        + 3.0 * mbuf[lax.rem(me + reps - 2, reps)]
        + mbuf[lax.rem(me + reps - 3, reps)]
    ) / 8.0
    mass_o[0] = mass_next
    mass_o[1] = jnp.sum(mbuf[...], axis=0)
    weight = mass_s[0]
    scale = (1.0 / (8.0 * mass_next))[0:1, :]

    def span_of(j):
        return pl.ds(pl.multiple_of(j * span, 128), span)

    def remote(src, dst, send, recv, target):
        return pltpu.make_async_remote_copy(
            src_ref=src, dst_ref=dst, send_sem=send, recv_sem=recv,
            device_id={"blk": target}, device_id_type=MESH,
        )

    def pair_copy(j):
        return remote(nb.at[j], eb.at[j], e_send.at[j], e_recv.at[j], partner)

    def odd_ahead(j):
        return remote(nb.at[j], cb.at[j], c1_send.at[j], c_recv.at[j], ahead)

    def odd_across(j):
        return remote(cb.at[j], cb.at[j], c_send.at[j], c_recv.at[j], partner)

    def even_ahead(j):
        return remote(eb.at[j], cb.at[j], c_send.at[j], c_recv.at[j], ahead)

    def sum_copy(j):
        return remote(sb.at[j], rb.at[j], s_send.at[j], r_recv.at[j], ahead)

    def outs(j):
        at = span_of(j)
        return (
            pltpu.make_async_copy(wgu.at[at, pl.ds(0, units)], gate_o.at[at, :], o_sem.at[0, j]),
            pltpu.make_async_copy(
                wgu.at[at, pl.ds(units, units)], up_o.at[at, :], o_sem.at[1, j]
            ),
            pltpu.make_async_copy(wdv.at[:, at], down_o.at[:, at], o_sem.at[2, j]),
        )

    def mix_step(t, carry):
        @pl.when(t < chunks)
        def _():
            j = t
            at = span_of(j)
            grads = lax.dot_general(
                xy[0, :, at], gpre[...], (((0,), (0,)), ((), ())), preferred_element_type=f32
            )
            numer = (weight * (wgu[at, :].astype(f32) - (step_size * inv_d) * grads)).astype(bf16)
            nb[j, 0] = numer[:, :units]
            nb[j, 1] = numer[:, units:]
            down_grad = jnp.dot(hid_t[...], xy[1, :, at], preferred_element_type=f32)
            down = (
                weight * (wdv[:, at].astype(f32) - (step_size * inv_h) * down_grad)
            ).astype(bf16)
            for b in range(span // units):
                nb[j, 2, b * units : (b + 1) * units, :] = down[:, b * units : (b + 1) * units]
            pair_copy(j).start()

            @pl.when(odd & (lax.rem(j, 2) == 1))
            def _():
                odd_ahead(j).start()

        @pl.when((t >= 2) & (t < chunks + 2))
        def _():
            j = t - 2
            pair_copy(j).wait_recv()

            @pl.when(even & (lax.rem(j, 2) == 0))
            def _():
                even_ahead(j).start()

            @pl.when(odd)
            def _():
                sb[j] = (3.0 * nb[j].astype(f32) + eb[j].astype(f32)).astype(bf16)
                sum_copy(j).start()

            @pl.when(odd & (lax.rem(j, 2) == 1))
            def _():
                odd_ahead(j).wait_recv()
                odd_across(j).start()

        @pl.when((t >= 4) & (t < chunks + 4) & even)
        def _():
            j = t - 4
            even_ahead(j).wait_recv()
            sb[j] = (
                3.0 * (nb[j].astype(f32) + eb[j].astype(f32)) + cb[j].astype(f32)
            ).astype(bf16)
            sum_copy(j).start()

        @pl.when(t >= 7)
        def _():
            j = t - 7
            sum_copy(j).wait_recv()
            at = span_of(j)
            near = jnp.where(odd, 3.0, 0.0).astype(f32)

            def mixed(i):
                total = nb[j, i].astype(f32) + near * eb[j, i].astype(f32)
                return ((total + rb[j, i].astype(f32)) * scale).astype(bf16)

            wgu[at, :units] = mixed(0)
            wgu[at, units:] = mixed(1)
            down = mixed(2)
            for b in range(span // units):
                here = pl.ds(pl.multiple_of(j * span + b * units, 128), units)
                wdv[:, here] = down[b * units : (b + 1) * units, :]
            for out in outs(j):
                out.start()

        return carry

    lax.fori_loop(0, chunks + 7, mix_step, 0)

    def drain_gather(p, carry):
        for a in range(2):
            own_copy(a, p).wait_send()
            for q in range(far):
                far_copy(a, q, p).wait_send()
                fwd_copy(a, q, p).wait_send()
        return carry

    lax.fori_loop(0, pieces, drain_gather, 0)

    def drain_mix(j, carry):
        pair_copy(j).wait_send()
        sum_copy(j).wait_send()

        @pl.when(odd & (lax.rem(j, 2) == 1))
        def _():
            odd_ahead(j).wait_send()
            odd_across(j).wait_send()

        @pl.when(even & (lax.rem(j, 2) == 0))
        def _():
            even_ahead(j).wait_send()

        for out in outs(j):
            out.wait()
        return carry

    lax.fori_loop(0, chunks, drain_mix, 0)


def on_device(reps, mp, tokens, cotangent, gate_weight, up_weight, down_weight, mass):
    rows, width = tokens.shape[1:]
    units = gate_weight.shape[2]
    pieces = largest_cut(width, 7)
    chunks = largest_cut(width, 14)
    span = width // chunks
    far = max(mp // 2 - 1, 1)
    dma = pltpu.SemaphoreType.DMA
    slab = pltpu.VMEM((chunks, 3, span, units), bf16)
    anywhere = pl.BlockSpec(memory_space=pl.ANY)
    vmem = pl.BlockSpec(memory_space=pltpu.VMEM)
    gate, up, down, masses = pl.pallas_call(
        functools.partial(kernel, reps, mp, pieces, chunks),
        out_shape=(
            jax.ShapeDtypeStruct((width, units), bf16),
            jax.ShapeDtypeStruct((width, units), bf16),
            jax.ShapeDtypeStruct((units, width), bf16),
            jax.ShapeDtypeStruct((2, 8, 128), f32),
        ),
        in_specs=[anywhere] * 5 + [pl.BlockSpec(memory_space=pltpu.SMEM), vmem],
        out_specs=(anywhere, anywhere, anywhere, vmem),
        scratch_shapes=[
            pltpu.VMEM((2, rows * mp, width), bf16),
            pltpu.VMEM((width, 2 * units), bf16),
            pltpu.VMEM((units, width), bf16),
            slab, slab, slab, slab, slab,
            pltpu.VMEM((reps, 8, 128), f32),
            pltpu.VMEM((rows * mp, 2 * units), f32),
            pltpu.VMEM((rows * mp, units), f32),
            pltpu.VMEM((rows * mp, 2 * units), bf16),
            pltpu.VMEM((units, rows * mp), bf16),
            dma((5,)),
            dma((2, pieces)), dma((2, pieces)),
            dma((2, far, pieces)), dma((2, far, pieces)),
            dma((2, far, pieces)), dma((2, far, pieces)),
            dma((reps,)), dma((reps,)),
            dma((chunks,)), dma((chunks,)), dma((chunks,)), dma((chunks,)),
            dma((chunks,)), dma((chunks,)), dma((chunks,)),
            dma((3, chunks)),
        ],
        compiler_params=pltpu.CompilerParams(
            collective_id=0, has_side_effects=True, vmem_limit_bytes=60 * 1024 * 1024
        ),
        name="push_step",
    )(
        tokens[0], cotangent[0], gate_weight[0], up_weight[0], down_weight[0],
        mass, jnp.broadcast_to(mass[0], (8, 128)),
    )
    return gate[None], up[None], down[None], masses[0, 0, :1], masses[1, 0, 0]


def solution(mesh):
    in_specs = (
        P("blk", "mp", None),
        P("blk", "mp", None),
        P("blk", None, "mp"),
        P("blk", None, "mp"),
        P("blk", "mp", None),
        P("blk"),
    )
    out_specs = (P("blk", None, "mp"), P("blk", None, "mp"), P("blk", "mp", None), P("blk"), P())
    return jax.shard_map(
        functools.partial(on_device, mesh.shape["blk"], mesh.shape["mp"]),
        mesh=mesh, in_specs=in_specs, out_specs=out_specs, check_vma=False,
    )
```

```python
import functools

import jax
import jax.numpy as jnp
from jax import lax
from jax.experimental import pallas as pl
from jax.experimental.pallas import tpu as pltpu
from jax.sharding import PartitionSpec as P

step_size = 0.5
lag_b, lag_c, lag_d = 2, 3, 6
MESH = pl.DeviceIdType.MESH
f32 = jnp.float32
bf16 = jnp.bfloat16


def largest_cut(width, most):
    return max(c for c in range(1, most + 1) if width % (c * 128) == 0)


def kernel(
    reps, mp, pieces, chunks,
    tok, cot, wg, wu, wd, mass_s, mass_v,
    gate_o, up_o, down_o, mass_o,
    xy, wgu, wdv, nb, eb, cb, sb, rb, mbuf, acc_gu, acc_h, gpre, hid_t,
    load_sem, own_send, own_recv, far_send, far_recv, fwd_send, fwd_recv,
    m_send, m_recv, e_send, e_recv, c1_send, c_send, c_recv, s_send, r_recv, o_sem,
):
    me = lax.axis_index("blk")
    my = lax.axis_index("mp")
    rows = tok.shape[0]
    width = tok.shape[1]
    units = wg.shape[1]
    inv_d = width ** (-0.5)
    inv_h = (units * mp) ** (-0.5)
    piece = width // pieces
    span = width // chunks
    far = mp // 2 - 1
    odd = lax.rem(me, 2) == 1
    even = lax.rem(me, 2) == 0
    partner = me + 1 - 2 * lax.rem(me, 2)
    ahead = lax.rem(me + 2, reps)
    sibling = my + 1 - 2 * lax.rem(my, 2)

    sources = (tok, cot)
    loads = [
        pltpu.make_async_copy(wg, wgu.at[:, pl.ds(0, units)], load_sem.at[0]),
        pltpu.make_async_copy(wu, wgu.at[:, pl.ds(units, units)], load_sem.at[1]),
        pltpu.make_async_copy(wd, wdv, load_sem.at[2]),
    ]
    mine = pl.ds(pl.multiple_of(my * rows, rows), rows)
    for a in range(2):
        loads.append(pltpu.make_async_copy(sources[a], xy.at[a, mine, :], load_sem.at[3 + a]))
    for load in loads:
        load.start()

    barrier = pltpu.get_barrier_semaphore()

    def greet_blk(d, carry):
        pl.semaphore_signal(
            barrier, inc=1, device_id={"blk": lax.rem(me + d, reps)}, device_id_type=MESH
        )
        return carry

    def greet_mp(d, carry):
        pl.semaphore_signal(
            barrier, inc=1, device_id={"mp": lax.rem(my + d, mp)}, device_id_type=MESH
        )
        return carry

    lax.fori_loop(1, reps, greet_blk, 0)
    lax.fori_loop(1, mp, greet_mp, 0)
    pl.semaphore_wait(barrier, reps - 1 + mp - 1)

    def cols_of(p):
        return pl.ds(pl.multiple_of(p * piece, 128), piece)

    def rows_of(owner):
        return pl.ds(pl.multiple_of(owner * rows, rows), rows)

    def own_copy(a, p):
        return pltpu.make_async_remote_copy(
            src_ref=sources[a].at[:, cols_of(p)],
            dst_ref=xy.at[a, mine, cols_of(p)],
            send_sem=own_send.at[a, p],
            recv_sem=own_recv.at[a, p],
            device_id={"mp": sibling},
            device_id_type=MESH,
        )

    def far_copy(a, q, p):
        return pltpu.make_async_remote_copy(
            src_ref=sources[a].at[:, cols_of(p)],
            dst_ref=xy.at[a, mine, cols_of(p)],
            send_sem=far_send.at[a, q, p],
            recv_sem=far_recv.at[a, q, p],
            device_id={"mp": lax.rem(my + 2 * (q + 1), mp)},
            device_id_type=MESH,
        )

    def fwd_copy(a, q, p):
        owner = lax.rem(my + mp - 2 * (q + 1), mp)
        block = xy.at[a, rows_of(owner), cols_of(p)]
        return pltpu.make_async_remote_copy(
            src_ref=block,
            dst_ref=block,
            send_sem=fwd_send.at[a, q, p],
            recv_sem=fwd_recv.at[a, q, p],
            device_id={"mp": sibling},
            device_id_type=MESH,
        )

    def issue(p, carry):
        for a in range(2):
            for q in range(far):
                far_copy(a, q, p).start()
            own_copy(a, p).start()
        return carry

    lax.fori_loop(0, pieces, issue, 0)

    def mass_copy(d):
        return pltpu.make_async_remote_copy(
            src_ref=mass_v,
            dst_ref=mbuf.at[me],
            send_sem=m_send.at[d],
            recv_sem=m_recv.at[d],
            device_id={"blk": lax.rem(me + d, reps)},
            device_id_type=MESH,
        )

    def mass_start(d, carry):
        mass_copy(d).start()
        return carry

    lax.fori_loop(1, reps, mass_start, 0)
    mbuf[me] = mass_v[...]

    acc_gu[...] = jnp.zeros_like(acc_gu)
    acc_h[...] = jnp.zeros_like(acc_h)
    for load in loads:
        load.wait()

    def gather_step(t, carry):
        @pl.when(t < pieces)
        def _():
            for a in range(2):
                for q in range(far):
                    far_copy(a, q, t).wait_recv()
                    fwd_copy(a, q, t).start()

        @pl.when(t >= 1)
        def _():
            p = t - 1
            for a in range(2):
                own_copy(a, p).wait_recv()
                for q in range(far):
                    fwd_copy(a, q, p).wait_recv()
            cols = cols_of(p)
            acc_gu[...] += jnp.dot(xy[0, :, cols], wgu[cols, :], preferred_element_type=f32)
            acc_h[...] += lax.dot_general(
                xy[1, :, cols], wdv[:, cols], (((1,), (1,)), ((), ())),
                preferred_element_type=f32,
            )

        return carry

    lax.fori_loop(0, pieces + 1, gather_step, 0)

    gate_pre = acc_gu[:, :units] * inv_d
    up_pre = acc_gu[:, units:] * inv_d
    sig = jax.nn.sigmoid(gate_pre)
    hidden = gate_pre * sig * up_pre
    hid_t[...] = hidden.T.astype(bf16)
    hidden_grad = acc_h[...] * inv_h
    gpre[:, :units] = (hidden_grad * up_pre * sig * (1.0 + gate_pre * (1.0 - sig))).astype(bf16)
    gpre[:, units:] = (hidden_grad * gate_pre * sig).astype(bf16)

    def mass_wait(d, carry):
        mass_copy(d).wait()
        return carry

    lax.fori_loop(1, reps, mass_wait, 0)
    mass_next = (
        mbuf[me]
        + 3.0 * mbuf[lax.rem(me + reps - 1, reps)]
        + 3.0 * mbuf[lax.rem(me + reps - 2, reps)]
        + mbuf[lax.rem(me + reps - 3, reps)]
    ) / 8.0
    mass_o[0] = mass_next
    mass_o[1] = jnp.sum(mbuf[...], axis=0)
    weight = mass_s[0]
    scale = (1.0 / (8.0 * mass_next))[0:1, :]

    def span_of(j):
        return pl.ds(pl.multiple_of(j * span, 128), span)

    def remote(src, dst, send, recv, target):
        return pltpu.make_async_remote_copy(
            src_ref=src, dst_ref=dst, send_sem=send, recv_sem=recv,
            device_id={"blk": target}, device_id_type=MESH,
        )

    def pair_copy(j):
        return remote(nb.at[j], eb.at[j], e_send.at[j], e_recv.at[j], partner)

    def odd_ahead(j):
        return remote(nb.at[j], cb.at[j], c1_send.at[j], c_recv.at[j], ahead)

    def odd_across(j):
        return remote(cb.at[j], eb.at[j], c_send.at[j], e_recv.at[j], partner)

    def even_ahead(j):
        return remote(eb.at[j], cb.at[j], c_send.at[j], c_recv.at[j], ahead)

    def sum_copy(j):
        return remote(sb.at[j], rb.at[j], s_send.at[j], r_recv.at[j], ahead)

    def outs(j):
        at = span_of(j)
        return (
            pltpu.make_async_copy(wgu.at[at, pl.ds(0, units)], gate_o.at[at, :], o_sem.at[0, j]),
            pltpu.make_async_copy(
                wgu.at[at, pl.ds(units, units)], up_o.at[at, :], o_sem.at[1, j]
            ),
            pltpu.make_async_copy(wdv.at[:, at], down_o.at[:, at], o_sem.at[2, j]),
        )

    def mix_step(t, carry):
        @pl.when(t < chunks)
        def _():
            j = t
            at = span_of(j)
            grads = lax.dot_general(
                xy[0, :, at], gpre[...], (((0,), (0,)), ((), ())), preferred_element_type=f32
            )
            numer = (weight * (wgu[at, :].astype(f32) - (step_size * inv_d) * grads)).astype(bf16)
            nb[j, 0] = numer[:, :units]
            nb[j, 1] = numer[:, units:]
            down_grad = jnp.dot(hid_t[...], xy[1, :, at], preferred_element_type=f32)
            down = (
                weight * (wdv[:, at].astype(f32) - (step_size * inv_h) * down_grad)
            ).astype(bf16)
            for b in range(span // units):
                nb[j, 2, b * units : (b + 1) * units, :] = down[:, b * units : (b + 1) * units]
            via_odd = lax.rem(j, 2) == 1

            @pl.when(odd & via_odd)
            def _():
                odd_ahead(j).start()

            @pl.when(even | jnp.logical_not(via_odd))
            def _():
                pair_copy(j).start()

        @pl.when((t >= lag_b) & (t < chunks + lag_b))
        def _():
            j = t - lag_b
            via_odd = lax.rem(j, 2) == 1

            @pl.when(odd)
            def _():
                pair_copy(j).wait_recv()
                sb[j] = (3.0 * nb[j].astype(f32) + eb[j].astype(f32)).astype(bf16)
                sum_copy(j).start()

            @pl.when(odd & via_odd)
            def _():
                odd_ahead(j).wait_recv()
                cb[j] = (3.0 * nb[j].astype(f32) + cb[j].astype(f32)).astype(bf16)
                odd_across(j).start()

            @pl.when(even & jnp.logical_not(via_odd))
            def _():
                pair_copy(j).wait_recv()
                even_ahead(j).start()

        @pl.when((t >= lag_c) & (t < chunks + lag_c) & even)
        def _():
            j = t - lag_c
            via_odd = lax.rem(j, 2) == 1

            @pl.when(via_odd)
            def _():
                odd_across(j).wait_recv()
                sb[j] = (3.0 * nb[j].astype(f32) + eb[j].astype(f32)).astype(bf16)

            @pl.when(jnp.logical_not(via_odd))
            def _():
                even_ahead(j).wait_recv()
                sb[j] = (
                    3.0 * (nb[j].astype(f32) + eb[j].astype(f32)) + cb[j].astype(f32)
                ).astype(bf16)

            sum_copy(j).start()

        @pl.when(t >= lag_d)
        def _():
            j = t - lag_d
            sum_copy(j).wait_recv()
            at = span_of(j)
            near = jnp.where(odd, 3.0, 0.0).astype(f32)

            def mixed(i):
                total = nb[j, i].astype(f32) + near * eb[j, i].astype(f32)
                return ((total + rb[j, i].astype(f32)) * scale).astype(bf16)

            wgu[at, :units] = mixed(0)
            wgu[at, units:] = mixed(1)
            down = mixed(2)
            for b in range(span // units):
                here = pl.ds(pl.multiple_of(j * span + b * units, 128), units)
                wdv[:, here] = down[b * units : (b + 1) * units, :]
            for out in outs(j):
                out.start()

        return carry

    lax.fori_loop(0, chunks + lag_d, mix_step, 0)

    def drain_gather(p, carry):
        for a in range(2):
            own_copy(a, p).wait_send()
            for q in range(far):
                far_copy(a, q, p).wait_send()
                fwd_copy(a, q, p).wait_send()
        return carry

    lax.fori_loop(0, pieces, drain_gather, 0)

    def drain_mix(j, carry):
        sum_copy(j).wait_send()

        @pl.when(even | (lax.rem(j, 2) == 0))
        def _():
            pair_copy(j).wait_send()

        @pl.when(odd & (lax.rem(j, 2) == 1))
        def _():
            odd_ahead(j).wait_send()
            odd_across(j).wait_send()

        @pl.when(even & (lax.rem(j, 2) == 0))
        def _():
            even_ahead(j).wait_send()

        for out in outs(j):
            out.wait()
        return carry

    lax.fori_loop(0, chunks, drain_mix, 0)


def on_device(reps, mp, tokens, cotangent, gate_weight, up_weight, down_weight, mass):
    rows, width = tokens.shape[1:]
    units = gate_weight.shape[2]
    pieces = largest_cut(width, 7)
    chunks = largest_cut(width, 28)
    span = width // chunks
    far = max(mp // 2 - 1, 1)
    dma = pltpu.SemaphoreType.DMA
    slab = pltpu.VMEM((chunks, 3, span, units), bf16)
    anywhere = pl.BlockSpec(memory_space=pl.ANY)
    vmem = pl.BlockSpec(memory_space=pltpu.VMEM)
    gate, up, down, masses = pl.pallas_call(
        functools.partial(kernel, reps, mp, pieces, chunks),
        out_shape=(
            jax.ShapeDtypeStruct((width, units), bf16),
            jax.ShapeDtypeStruct((width, units), bf16),
            jax.ShapeDtypeStruct((units, width), bf16),
            jax.ShapeDtypeStruct((2, 8, 128), f32),
        ),
        in_specs=[anywhere] * 5 + [pl.BlockSpec(memory_space=pltpu.SMEM), vmem],
        out_specs=(anywhere, anywhere, anywhere, vmem),
        scratch_shapes=[
            pltpu.VMEM((2, rows * mp, width), bf16),
            pltpu.VMEM((width, 2 * units), bf16),
            pltpu.VMEM((units, width), bf16),
            slab, slab, slab, slab, slab,
            pltpu.VMEM((reps, 8, 128), f32),
            pltpu.VMEM((rows * mp, 2 * units), f32),
            pltpu.VMEM((rows * mp, units), f32),
            pltpu.VMEM((rows * mp, 2 * units), bf16),
            pltpu.VMEM((units, rows * mp), bf16),
            dma((5,)),
            dma((2, pieces)), dma((2, pieces)),
            dma((2, far, pieces)), dma((2, far, pieces)),
            dma((2, far, pieces)), dma((2, far, pieces)),
            dma((reps,)), dma((reps,)),
            dma((chunks,)), dma((chunks,)), dma((chunks,)), dma((chunks,)),
            dma((chunks,)), dma((chunks,)), dma((chunks,)),
            dma((3, chunks)),
        ],
        compiler_params=pltpu.CompilerParams(
            collective_id=0, has_side_effects=True, vmem_limit_bytes=48 * 1024 * 1024
        ),
        name="push_step",
    )(
        tokens[0], cotangent[0], gate_weight[0], up_weight[0], down_weight[0],
        mass, jnp.broadcast_to(mass[0], (8, 128)),
    )
    return gate[None], up[None], down[None], masses[0, 0, :1], masses[1, 0, 0]


def solution(mesh):
    in_specs = (
        P("blk", "mp", None),
        P("blk", "mp", None),
        P("blk", None, "mp"),
        P("blk", None, "mp"),
        P("blk", "mp", None),
        P("blk"),
    )
    out_specs = (P("blk", None, "mp"), P("blk", None, "mp"), P("blk", "mp", None), P("blk"), P())
    return jax.shard_map(
        functools.partial(on_device, mesh.shape["blk"], mesh.shape["mp"]),
        mesh=mesh, in_specs=in_specs, out_specs=out_specs, check_vma=False,
    )
```

```python
import functools

import jax
import jax.numpy as jnp
from jax import lax
from jax.experimental import pallas as pl
from jax.experimental.pallas import tpu as pltpu
from jax.sharding import PartitionSpec as P

step_size = 0.5
lag_b, lag_c, lag_d = 3, 4, 8
MESH = pl.DeviceIdType.MESH
f32 = jnp.float32
bf16 = jnp.bfloat16


def largest_cut(width, most):
    return max(c for c in range(1, most + 1) if width % (c * 128) == 0)


def kernel(
    reps, mp, pieces, chunks,
    tok, cot, wg, wu, wd, mass_s, mass_v,
    gate_o, up_o, down_o, mass_o,
    xy, wgu, wdv, nb, eb, cb, sb, rb, mbuf, acc_gu, acc_h, gpre, hid_t,
    load_sem, own_send, own_recv, far_send, far_recv, fwd_send, fwd_recv,
    m_send, m_recv, e_send, e_recv, c1_send, c_send, c_recv, s_send, r_recv, o_sem,
):
    me = lax.axis_index("blk")
    my = lax.axis_index("mp")
    rows = tok.shape[0]
    width = tok.shape[1]
    units = wg.shape[1]
    inv_d = width ** (-0.5)
    inv_h = (units * mp) ** (-0.5)
    piece = width // pieces
    span = width // chunks
    far = mp // 2 - 1
    odd = lax.rem(me, 2) == 1
    even = lax.rem(me, 2) == 0
    partner = me + 1 - 2 * lax.rem(me, 2)
    ahead = lax.rem(me + 2, reps)
    sibling = my + 1 - 2 * lax.rem(my, 2)

    sources = (tok, cot)
    loads = [
        pltpu.make_async_copy(wg, wgu.at[:, pl.ds(0, units)], load_sem.at[0]),
        pltpu.make_async_copy(wu, wgu.at[:, pl.ds(units, units)], load_sem.at[1]),
        pltpu.make_async_copy(wd, wdv, load_sem.at[2]),
    ]
    mine = pl.ds(pl.multiple_of(my * rows, rows), rows)
    for a in range(2):
        loads.append(pltpu.make_async_copy(sources[a], xy.at[a, mine, :], load_sem.at[3 + a]))
    for load in loads:
        load.start()

    barrier = pltpu.get_barrier_semaphore()

    def greet_blk(d, carry):
        pl.semaphore_signal(
            barrier, inc=1, device_id={"blk": lax.rem(me + d, reps)}, device_id_type=MESH
        )
        return carry

    def greet_mp(d, carry):
        pl.semaphore_signal(
            barrier, inc=1, device_id={"mp": lax.rem(my + d, mp)}, device_id_type=MESH
        )
        return carry

    lax.fori_loop(1, reps, greet_blk, 0)
    lax.fori_loop(1, mp, greet_mp, 0)
    pl.semaphore_wait(barrier, reps - 1 + mp - 1)

    def cols_of(p):
        return pl.ds(pl.multiple_of(p * piece, 128), piece)

    def rows_of(owner):
        return pl.ds(pl.multiple_of(owner * rows, rows), rows)

    def own_copy(a, p):
        return pltpu.make_async_remote_copy(
            src_ref=sources[a].at[:, cols_of(p)],
            dst_ref=xy.at[a, mine, cols_of(p)],
            send_sem=own_send.at[a, p],
            recv_sem=own_recv.at[a, p],
            device_id={"mp": sibling},
            device_id_type=MESH,
        )

    def far_copy(a, q, p):
        return pltpu.make_async_remote_copy(
            src_ref=sources[a].at[:, cols_of(p)],
            dst_ref=xy.at[a, mine, cols_of(p)],
            send_sem=far_send.at[a, q, p],
            recv_sem=far_recv.at[a, q, p],
            device_id={"mp": lax.rem(my + 2 * (q + 1), mp)},
            device_id_type=MESH,
        )

    def fwd_copy(a, q, p):
        owner = lax.rem(my + mp - 2 * (q + 1), mp)
        block = xy.at[a, rows_of(owner), cols_of(p)]
        return pltpu.make_async_remote_copy(
            src_ref=block,
            dst_ref=block,
            send_sem=fwd_send.at[a, q, p],
            recv_sem=fwd_recv.at[a, q, p],
            device_id={"mp": sibling},
            device_id_type=MESH,
        )

    def issue(p, carry):
        for a in range(2):
            for q in range(far):
                far_copy(a, q, p).start()
            own_copy(a, p).start()
        return carry

    lax.fori_loop(0, pieces, issue, 0)

    def mass_copy(d):
        return pltpu.make_async_remote_copy(
            src_ref=mass_v,
            dst_ref=mbuf.at[me],
            send_sem=m_send.at[d],
            recv_sem=m_recv.at[d],
            device_id={"blk": lax.rem(me + d, reps)},
            device_id_type=MESH,
        )

    def mass_start(d, carry):
        mass_copy(d).start()
        return carry

    lax.fori_loop(1, reps, mass_start, 0)
    mbuf[me] = mass_v[...]

    acc_gu[...] = jnp.zeros_like(acc_gu)
    acc_h[...] = jnp.zeros_like(acc_h)
    for load in loads:
        load.wait()

    def gather_step(t, carry):
        @pl.when(t < pieces)
        def _():
            for a in range(2):
                for q in range(far):
                    far_copy(a, q, t).wait_recv()
                    fwd_copy(a, q, t).start()

        @pl.when(t >= 1)
        def _():
            p = t - 1
            for a in range(2):
                own_copy(a, p).wait_recv()
                for q in range(far):
                    fwd_copy(a, q, p).wait_recv()
            cols = cols_of(p)
            acc_gu[...] += jnp.dot(xy[0, :, cols], wgu[cols, :], preferred_element_type=f32)
            acc_h[...] += lax.dot_general(
                xy[1, :, cols], wdv[:, cols], (((1,), (1,)), ((), ())),
                preferred_element_type=f32,
            )

        return carry

    lax.fori_loop(0, pieces + 1, gather_step, 0)

    gate_pre = acc_gu[:, :units] * inv_d
    up_pre = acc_gu[:, units:] * inv_d
    sig = jax.nn.sigmoid(gate_pre)
    hidden = gate_pre * sig * up_pre
    hid_t[...] = hidden.T.astype(bf16)
    hidden_grad = acc_h[...] * inv_h
    gpre[:, :units] = (hidden_grad * up_pre * sig * (1.0 + gate_pre * (1.0 - sig))).astype(bf16)
    gpre[:, units:] = (hidden_grad * gate_pre * sig).astype(bf16)

    def mass_wait(d, carry):
        mass_copy(d).wait()
        return carry

    lax.fori_loop(1, reps, mass_wait, 0)
    mass_next = (
        mbuf[me]
        + 3.0 * mbuf[lax.rem(me + reps - 1, reps)]
        + 3.0 * mbuf[lax.rem(me + reps - 2, reps)]
        + mbuf[lax.rem(me + reps - 3, reps)]
    ) / 8.0
    mass_o[0] = mass_next
    mass_o[1] = jnp.sum(mbuf[...], axis=0)
    weight = mass_s[0]
    scale = (1.0 / (8.0 * mass_next))[0:1, :]

    def through_odd(j):
        return (lax.rem(j, 2) == 1) | (j == chunks // 2)

    def span_of(j):
        return pl.ds(pl.multiple_of(j * span, 128), span)

    def remote(src, dst, send, recv, target):
        return pltpu.make_async_remote_copy(
            src_ref=src, dst_ref=dst, send_sem=send, recv_sem=recv,
            device_id={"blk": target}, device_id_type=MESH,
        )

    def pair_copy(j):
        return remote(nb.at[j], eb.at[j], e_send.at[j], e_recv.at[j], partner)

    def odd_ahead(j):
        return remote(nb.at[j], cb.at[j], c1_send.at[j], c_recv.at[j], ahead)

    def odd_across(j):
        return remote(cb.at[j], eb.at[j], c_send.at[j], e_recv.at[j], partner)

    def even_ahead(j):
        return remote(eb.at[j], cb.at[j], c_send.at[j], c_recv.at[j], ahead)

    def sum_copy(j):
        return remote(sb.at[j], rb.at[j], s_send.at[j], r_recv.at[j], ahead)

    def outs(j):
        at = span_of(j)
        return (
            pltpu.make_async_copy(wgu.at[at, pl.ds(0, units)], gate_o.at[at, :], o_sem.at[0, j]),
            pltpu.make_async_copy(
                wgu.at[at, pl.ds(units, units)], up_o.at[at, :], o_sem.at[1, j]
            ),
            pltpu.make_async_copy(wdv.at[:, at], down_o.at[:, at], o_sem.at[2, j]),
        )

    def mix_step(t, carry):
        @pl.when(t < chunks)
        def _():
            j = t
            at = span_of(j)
            grads = lax.dot_general(
                xy[0, :, at], gpre[...], (((0,), (0,)), ((), ())), preferred_element_type=f32
            )
            numer = (weight * (wgu[at, :].astype(f32) - (step_size * inv_d) * grads)).astype(bf16)
            nb[j, 0] = numer[:, :units]
            nb[j, 1] = numer[:, units:]
            down_grad = jnp.dot(hid_t[...], xy[1, :, at], preferred_element_type=f32)
            down = (
                weight * (wdv[:, at].astype(f32) - (step_size * inv_h) * down_grad)
            ).astype(bf16)
            for b in range(span // units):
                nb[j, 2, b * units : (b + 1) * units, :] = down[:, b * units : (b + 1) * units]
            via_odd = through_odd(j)

            @pl.when(odd & via_odd)
            def _():
                odd_ahead(j).start()

            @pl.when(even | jnp.logical_not(via_odd))
            def _():
                pair_copy(j).start()

        @pl.when((t >= lag_b) & (t < chunks + lag_b))
        def _():
            j = t - lag_b
            via_odd = through_odd(j)

            @pl.when(odd)
            def _():
                pair_copy(j).wait_recv()
                sb[j] = (3.0 * nb[j].astype(f32) + eb[j].astype(f32)).astype(bf16)
                sum_copy(j).start()

            @pl.when(odd & via_odd)
            def _():
                odd_ahead(j).wait_recv()
                cb[j] = (3.0 * nb[j].astype(f32) + cb[j].astype(f32)).astype(bf16)
                odd_across(j).start()

            @pl.when(even & jnp.logical_not(via_odd))
            def _():
                pair_copy(j).wait_recv()
                even_ahead(j).start()

        @pl.when((t >= lag_c) & (t < chunks + lag_c) & even)
        def _():
            j = t - lag_c
            via_odd = through_odd(j)

            @pl.when(via_odd)
            def _():
                odd_across(j).wait_recv()
                sb[j] = (3.0 * nb[j].astype(f32) + eb[j].astype(f32)).astype(bf16)

            @pl.when(jnp.logical_not(via_odd))
            def _():
                even_ahead(j).wait_recv()
                sb[j] = (
                    3.0 * (nb[j].astype(f32) + eb[j].astype(f32)) + cb[j].astype(f32)
                ).astype(bf16)

            sum_copy(j).start()

        @pl.when(t >= lag_d)
        def _():
            j = t - lag_d
            sum_copy(j).wait_recv()
            at = span_of(j)
            near = jnp.where(odd, 3.0, 0.0).astype(f32)

            def mixed(i):
                total = nb[j, i].astype(f32) + near * eb[j, i].astype(f32)
                return ((total + rb[j, i].astype(f32)) * scale).astype(bf16)

            wgu[at, :units] = mixed(0)
            wgu[at, units:] = mixed(1)
            down = mixed(2)
            for b in range(span // units):
                here = pl.ds(pl.multiple_of(j * span + b * units, 128), units)
                wdv[:, here] = down[b * units : (b + 1) * units, :]
            for out in outs(j):
                out.start()

        return carry

    lax.fori_loop(0, chunks + lag_d, mix_step, 0)

    def drain_gather(p, carry):
        for a in range(2):
            own_copy(a, p).wait_send()
            for q in range(far):
                far_copy(a, q, p).wait_send()
                fwd_copy(a, q, p).wait_send()
        return carry

    lax.fori_loop(0, pieces, drain_gather, 0)

    def drain_mix(j, carry):
        sum_copy(j).wait_send()

        @pl.when(even | jnp.logical_not(through_odd(j)))
        def _():
            pair_copy(j).wait_send()

        @pl.when(odd & through_odd(j))
        def _():
            odd_ahead(j).wait_send()
            odd_across(j).wait_send()

        @pl.when(even & jnp.logical_not(through_odd(j)))
        def _():
            even_ahead(j).wait_send()

        for out in outs(j):
            out.wait()
        return carry

    lax.fori_loop(0, chunks, drain_mix, 0)


def on_device(reps, mp, tokens, cotangent, gate_weight, up_weight, down_weight, mass):
    rows, width = tokens.shape[1:]
    units = gate_weight.shape[2]
    pieces = largest_cut(width, 7)
    chunks = largest_cut(width, 28)
    span = width // chunks
    far = max(mp // 2 - 1, 1)
    dma = pltpu.SemaphoreType.DMA
    slab = pltpu.VMEM((chunks, 3, span, units), bf16)
    anywhere = pl.BlockSpec(memory_space=pl.ANY)
    vmem = pl.BlockSpec(memory_space=pltpu.VMEM)
    gate, up, down, masses = pl.pallas_call(
        functools.partial(kernel, reps, mp, pieces, chunks),
        out_shape=(
            jax.ShapeDtypeStruct((width, units), bf16),
            jax.ShapeDtypeStruct((width, units), bf16),
            jax.ShapeDtypeStruct((units, width), bf16),
            jax.ShapeDtypeStruct((2, 8, 128), f32),
        ),
        in_specs=[anywhere] * 5 + [pl.BlockSpec(memory_space=pltpu.SMEM), vmem],
        out_specs=(anywhere, anywhere, anywhere, vmem),
        scratch_shapes=[
            pltpu.VMEM((2, rows * mp, width), bf16),
            pltpu.VMEM((width, 2 * units), bf16),
            pltpu.VMEM((units, width), bf16),
            slab, slab, slab, slab, slab,
            pltpu.VMEM((reps, 8, 128), f32),
            pltpu.VMEM((rows * mp, 2 * units), f32),
            pltpu.VMEM((rows * mp, units), f32),
            pltpu.VMEM((rows * mp, 2 * units), bf16),
            pltpu.VMEM((units, rows * mp), bf16),
            dma((5,)),
            dma((2, pieces)), dma((2, pieces)),
            dma((2, far, pieces)), dma((2, far, pieces)),
            dma((2, far, pieces)), dma((2, far, pieces)),
            dma((reps,)), dma((reps,)),
            dma((chunks,)), dma((chunks,)), dma((chunks,)), dma((chunks,)),
            dma((chunks,)), dma((chunks,)), dma((chunks,)),
            dma((3, chunks)),
        ],
        compiler_params=pltpu.CompilerParams(
            collective_id=0, has_side_effects=True, vmem_limit_bytes=53 * 1024 * 1024
        ),
        name="push_step",
    )(
        tokens[0], cotangent[0], gate_weight[0], up_weight[0], down_weight[0],
        mass, jnp.broadcast_to(mass[0], (8, 128)),
    )
    return gate[None], up[None], down[None], masses[0, 0, :1], masses[1, 0, 0]


def solution(mesh):
    in_specs = (
        P("blk", "mp", None),
        P("blk", "mp", None),
        P("blk", None, "mp"),
        P("blk", None, "mp"),
        P("blk", "mp", None),
        P("blk"),
    )
    out_specs = (P("blk", None, "mp"), P("blk", None, "mp"), P("blk", "mp", None), P("blk"), P())
    return jax.shard_map(
        functools.partial(on_device, mesh.shape["blk"], mesh.shape["mp"]),
        mesh=mesh, in_specs=in_specs, out_specs=out_specs, check_vma=False,
    )
```

```python
import functools

import jax
import jax.numpy as jnp
from jax import lax
from jax.experimental import pallas as pl
from jax.experimental.pallas import tpu as pltpu
from jax.sharding import PartitionSpec as P

step_size = 0.5
lag_b, lag_c, lag_d = 3, 4, 8
MESH = pl.DeviceIdType.MESH
f32 = jnp.float32
bf16 = jnp.bfloat16


def largest_cut(width, most):
    return max(c for c in range(1, most + 1) if width % (c * 128) == 0)


def kernel(
    reps, mp, pieces, chunks,
    tok, cot, wg, wu, wd, mass_s, mass_v,
    gate_o, up_o, down_o, mass_o,
    xy, wgu, wdv, nb, eb, cb, sb, rb, mbuf, acc_gu, acc_h, gpre, hid_t,
    load_sem, own_send, own_recv, far_send, far_recv, fwd_send, fwd_recv,
    m_send, m_recv, e_send, e_recv, c1_send, c_send, c_recv, s_send, r_recv, o_sem,
):
    me = lax.axis_index("blk")
    my = lax.axis_index("mp")
    rows = tok.shape[0]
    width = tok.shape[1]
    units = wg.shape[1]
    inv_d = width ** (-0.5)
    inv_h = (units * mp) ** (-0.5)
    piece = width // pieces
    span = width // chunks
    far = mp // 2 - 1
    odd = lax.rem(me, 2) == 1
    even = lax.rem(me, 2) == 0
    partner = me + 1 - 2 * lax.rem(me, 2)
    ahead = lax.rem(me + 2, reps)
    sibling = my + 1 - 2 * lax.rem(my, 2)

    sources = (tok, cot)
    loads = [
        pltpu.make_async_copy(wg, wgu.at[:, pl.ds(0, units)], load_sem.at[0]),
        pltpu.make_async_copy(wu, wgu.at[:, pl.ds(units, units)], load_sem.at[1]),
        pltpu.make_async_copy(wd, wdv, load_sem.at[2]),
    ]
    mine = pl.ds(pl.multiple_of(my * rows, rows), rows)
    for a in range(2):
        loads.append(pltpu.make_async_copy(sources[a], xy.at[a, mine, :], load_sem.at[3 + a]))
    for load in loads:
        load.start()

    barrier = pltpu.get_barrier_semaphore()

    def greet_blk(d, carry):
        pl.semaphore_signal(
            barrier, inc=1, device_id={"blk": lax.rem(me + d, reps)}, device_id_type=MESH
        )
        return carry

    def greet_mp(d, carry):
        pl.semaphore_signal(
            barrier, inc=1, device_id={"mp": lax.rem(my + d, mp)}, device_id_type=MESH
        )
        return carry

    lax.fori_loop(1, reps, greet_blk, 0)
    lax.fori_loop(1, mp, greet_mp, 0)
    pl.semaphore_wait(barrier, reps - 1 + mp - 1)

    def cols_of(p):
        return pl.ds(pl.multiple_of(p * piece, 128), piece)

    def rows_of(owner):
        return pl.ds(pl.multiple_of(owner * rows, rows), rows)

    def own_copy(a, p):
        return pltpu.make_async_remote_copy(
            src_ref=sources[a].at[:, cols_of(p)],
            dst_ref=xy.at[a, mine, cols_of(p)],
            send_sem=own_send.at[a, p],
            recv_sem=own_recv.at[a, p],
            device_id={"mp": sibling},
            device_id_type=MESH,
        )

    def far_copy(a, q, p):
        return pltpu.make_async_remote_copy(
            src_ref=sources[a].at[:, cols_of(p)],
            dst_ref=xy.at[a, mine, cols_of(p)],
            send_sem=far_send.at[a, q, p],
            recv_sem=far_recv.at[a, q, p],
            device_id={"mp": lax.rem(my + 2 * (q + 1), mp)},
            device_id_type=MESH,
        )

    def fwd_copy(a, q, p):
        owner = lax.rem(my + mp - 2 * (q + 1), mp)
        block = xy.at[a, rows_of(owner), cols_of(p)]
        return pltpu.make_async_remote_copy(
            src_ref=block,
            dst_ref=block,
            send_sem=fwd_send.at[a, q, p],
            recv_sem=fwd_recv.at[a, q, p],
            device_id={"mp": sibling},
            device_id_type=MESH,
        )

    def issue(p, carry):
        for a in range(2):
            for q in range(far):
                far_copy(a, q, p).start()
            own_copy(a, p).start()
        return carry

    lax.fori_loop(0, pieces, issue, 0)

    def mass_copy(d):
        return pltpu.make_async_remote_copy(
            src_ref=mass_v,
            dst_ref=mbuf.at[me],
            send_sem=m_send.at[d],
            recv_sem=m_recv.at[d],
            device_id={"blk": lax.rem(me + d, reps)},
            device_id_type=MESH,
        )

    def mass_start(d, carry):
        mass_copy(d).start()
        return carry

    lax.fori_loop(1, reps, mass_start, 0)
    mbuf[me] = mass_v[...]

    acc_gu[...] = jnp.zeros_like(acc_gu)
    acc_h[...] = jnp.zeros_like(acc_h)
    for load in loads:
        load.wait()

    def gather_step(t, carry):
        @pl.when(t < pieces)
        def _():
            for a in range(2):
                for q in range(far):
                    far_copy(a, q, t).wait_recv()
                    fwd_copy(a, q, t).start()

        @pl.when(t >= 1)
        def _():
            p = t - 1
            for a in range(2):
                own_copy(a, p).wait_recv()
                for q in range(far):
                    fwd_copy(a, q, p).wait_recv()
            cols = cols_of(p)
            acc_gu[...] += jnp.dot(xy[0, :, cols], wgu[cols, :], preferred_element_type=f32)
            acc_h[...] += lax.dot_general(
                xy[1, :, cols], wdv[:, cols], (((1,), (1,)), ((), ())),
                preferred_element_type=f32,
            )

        return carry

    lax.fori_loop(0, pieces + 1, gather_step, 0)

    gate_pre = acc_gu[:, :units] * inv_d
    up_pre = acc_gu[:, units:] * inv_d
    sig = jax.nn.sigmoid(gate_pre)
    hidden = gate_pre * sig * up_pre
    hid_t[...] = hidden.T.astype(bf16)
    hidden_grad = acc_h[...] * inv_h
    gpre[:, :units] = (hidden_grad * up_pre * sig * (1.0 + gate_pre * (1.0 - sig))).astype(bf16)
    gpre[:, units:] = (hidden_grad * gate_pre * sig).astype(bf16)

    def mass_wait(d, carry):
        mass_copy(d).wait()
        return carry

    lax.fori_loop(1, reps, mass_wait, 0)
    mass_next = (
        mbuf[me]
        + 3.0 * mbuf[lax.rem(me + reps - 1, reps)]
        + 3.0 * mbuf[lax.rem(me + reps - 2, reps)]
        + mbuf[lax.rem(me + reps - 3, reps)]
    ) / 8.0
    mass_o[0] = mass_next
    mass_o[1] = jnp.sum(mbuf[...], axis=0)
    weight = mass_s[0]
    scale = (1.0 / (8.0 * mass_next))[0:1, :]

    def through_odd(j):
        return (lax.rem(j, 2) == 1) | (j == chunks // 2)

    def span_of(j):
        return pl.ds(pl.multiple_of(j * span, 128), span)

    def remote(src, dst, send, recv, target):
        return pltpu.make_async_remote_copy(
            src_ref=src, dst_ref=dst, send_sem=send, recv_sem=recv,
            device_id={"blk": target}, device_id_type=MESH,
        )

    def pair_copy(j):
        return remote(nb.at[j], eb.at[j], e_send.at[j], e_recv.at[j], partner)

    def odd_ahead(j):
        return remote(nb.at[j], cb.at[j], c1_send.at[j], c_recv.at[j], ahead)

    def odd_across(j):
        return remote(cb.at[j], eb.at[j], c_send.at[j], e_recv.at[j], partner)

    def even_ahead(j):
        return remote(eb.at[j], cb.at[j], c_send.at[j], c_recv.at[j], ahead)

    def sum_copy(j):
        return remote(sb.at[j], rb.at[j], s_send.at[j], r_recv.at[j], ahead)

    def outs(j):
        at = span_of(j)
        return (
            pltpu.make_async_copy(wgu.at[at, pl.ds(0, units)], gate_o.at[at, :], o_sem.at[0, j]),
            pltpu.make_async_copy(
                wgu.at[at, pl.ds(units, units)], up_o.at[at, :], o_sem.at[1, j]
            ),
            pltpu.make_async_copy(wdv.at[:, at], down_o.at[:, at], o_sem.at[2, j]),
        )

    def mix_step(t, carry):
        @pl.when(t < chunks)
        def _():
            j = t
            at = span_of(j)
            grads = lax.dot_general(
                xy[0, :, at], gpre[...], (((0,), (0,)), ((), ())), preferred_element_type=f32
            )
            numer = (weight * (wgu[at, :].astype(f32) - (step_size * inv_d) * grads)).astype(bf16)
            nb[j, 0] = numer[:, :units]
            nb[j, 1] = numer[:, units:]
            down_grad = jnp.dot(hid_t[...], xy[1, :, at], preferred_element_type=f32)
            down = (
                weight * (wdv[:, at].astype(f32) - (step_size * inv_h) * down_grad)
            ).astype(bf16)
            for b in range(span // units):
                nb[j, 2, b * units : (b + 1) * units, :] = down[:, b * units : (b + 1) * units]
            via_odd = through_odd(j)

            @pl.when(odd & via_odd)
            def _():
                odd_ahead(j).start()

            @pl.when(even | jnp.logical_not(via_odd))
            def _():
                pair_copy(j).start()

        @pl.when((t >= lag_b) & (t < chunks + lag_b))
        def _():
            j = t - lag_b
            via_odd = through_odd(j)

            @pl.when(odd & via_odd)
            def _():
                odd_ahead(j).wait_recv()
                cb[j] = (3.0 * nb[j].astype(f32) + cb[j].astype(f32)).astype(bf16)
                odd_across(j).start()

            @pl.when(odd)
            def _():
                pair_copy(j).wait_recv()
                sb[j] = (3.0 * nb[j].astype(f32) + eb[j].astype(f32)).astype(bf16)
                sum_copy(j).start()

            @pl.when(even & jnp.logical_not(via_odd))
            def _():
                pair_copy(j).wait_recv()
                even_ahead(j).start()

        @pl.when((t >= lag_c) & (t < chunks + lag_c) & even)
        def _():
            j = t - lag_c
            via_odd = through_odd(j)

            @pl.when(via_odd)
            def _():
                odd_across(j).wait_recv()
                sb[j] = (3.0 * nb[j].astype(f32) + eb[j].astype(f32)).astype(bf16)

            @pl.when(jnp.logical_not(via_odd))
            def _():
                even_ahead(j).wait_recv()
                sb[j] = (
                    3.0 * (nb[j].astype(f32) + eb[j].astype(f32)) + cb[j].astype(f32)
                ).astype(bf16)

            sum_copy(j).start()

        @pl.when(t >= lag_d)
        def _():
            j = t - lag_d
            sum_copy(j).wait_recv()
            at = span_of(j)
            near = jnp.where(odd, 3.0, 0.0).astype(f32)

            def mixed(i):
                total = nb[j, i].astype(f32) + near * eb[j, i].astype(f32)
                return ((total + rb[j, i].astype(f32)) * scale).astype(bf16)

            wgu[at, :units] = mixed(0)
            wgu[at, units:] = mixed(1)
            down = mixed(2)
            for b in range(span // units):
                here = pl.ds(pl.multiple_of(j * span + b * units, 128), units)
                wdv[:, here] = down[b * units : (b + 1) * units, :]
            for out in outs(j):
                out.start()

        return carry

    lax.fori_loop(0, chunks + lag_d, mix_step, 0)

    def drain_gather(p, carry):
        for a in range(2):
            own_copy(a, p).wait_send()
            for q in range(far):
                far_copy(a, q, p).wait_send()
                fwd_copy(a, q, p).wait_send()
        return carry

    lax.fori_loop(0, pieces, drain_gather, 0)

    def drain_mix(j, carry):
        sum_copy(j).wait_send()

        @pl.when(even | jnp.logical_not(through_odd(j)))
        def _():
            pair_copy(j).wait_send()

        @pl.when(odd & through_odd(j))
        def _():
            odd_ahead(j).wait_send()
            odd_across(j).wait_send()

        @pl.when(even & jnp.logical_not(through_odd(j)))
        def _():
            even_ahead(j).wait_send()

        for out in outs(j):
            out.wait()
        return carry

    lax.fori_loop(0, chunks, drain_mix, 0)


def on_device(reps, mp, tokens, cotangent, gate_weight, up_weight, down_weight, mass):
    rows, width = tokens.shape[1:]
    units = gate_weight.shape[2]
    pieces = largest_cut(width, 7)
    chunks = largest_cut(width, 28)
    span = width // chunks
    far = max(mp // 2 - 1, 1)
    dma = pltpu.SemaphoreType.DMA
    slab = pltpu.VMEM((chunks, 3, span, units), bf16)
    anywhere = pl.BlockSpec(memory_space=pl.ANY)
    vmem = pl.BlockSpec(memory_space=pltpu.VMEM)
    gate, up, down, masses = pl.pallas_call(
        functools.partial(kernel, reps, mp, pieces, chunks),
        out_shape=(
            jax.ShapeDtypeStruct((width, units), bf16),
            jax.ShapeDtypeStruct((width, units), bf16),
            jax.ShapeDtypeStruct((units, width), bf16),
            jax.ShapeDtypeStruct((2, 8, 128), f32),
        ),
        in_specs=[anywhere] * 5 + [pl.BlockSpec(memory_space=pltpu.SMEM), vmem],
        out_specs=(anywhere, anywhere, anywhere, vmem),
        scratch_shapes=[
            pltpu.VMEM((2, rows * mp, width), bf16),
            pltpu.VMEM((width, 2 * units), bf16),
            pltpu.VMEM((units, width), bf16),
            slab, slab, slab, slab, slab,
            pltpu.VMEM((reps, 8, 128), f32),
            pltpu.VMEM((rows * mp, 2 * units), f32),
            pltpu.VMEM((rows * mp, units), f32),
            pltpu.VMEM((rows * mp, 2 * units), bf16),
            pltpu.VMEM((units, rows * mp), bf16),
            dma((5,)),
            dma((2, pieces)), dma((2, pieces)),
            dma((2, far, pieces)), dma((2, far, pieces)),
            dma((2, far, pieces)), dma((2, far, pieces)),
            dma((reps,)), dma((reps,)),
            dma((chunks,)), dma((chunks,)), dma((chunks,)), dma((chunks,)),
            dma((chunks,)), dma((chunks,)), dma((chunks,)),
            dma((3, chunks)),
        ],
        compiler_params=pltpu.CompilerParams(
            collective_id=0, has_side_effects=True, vmem_limit_bytes=53 * 1024 * 1024
        ),
        name="push_step",
    )(
        tokens[0], cotangent[0], gate_weight[0], up_weight[0], down_weight[0],
        mass, jnp.broadcast_to(mass[0], (8, 128)),
    )
    return gate[None], up[None], down[None], masses[0, 0, :1], masses[1, 0, 0]


def solution(mesh):
    in_specs = (
        P("blk", "mp", None),
        P("blk", "mp", None),
        P("blk", None, "mp"),
        P("blk", None, "mp"),
        P("blk", "mp", None),
        P("blk"),
    )
    out_specs = (P("blk", None, "mp"), P("blk", None, "mp"), P("blk", "mp", None), P("blk"), P())
    return jax.shard_map(
        functools.partial(on_device, mesh.shape["blk"], mesh.shape["mp"]),
        mesh=mesh, in_specs=in_specs, out_specs=out_specs, check_vma=False,
    )
```
